32 devices in a mesh: sec: 8 (over y, x, core), img: 4 (over z).
Axes of the slice: x: 2, y: 2, z: 4, core: 2. Of those that a mesh axis runs over, the one named last changes fastest.
Arguments:
- saved_last: bfloat16 [8, 4, 4, 21, 21, 384], P('sec', None, 'img'), may hold values from -6 to 6
- saved_older: bfloat16 [8, 4, 4, 21, 21, 384], P('sec', None, 'img'), may hold values from -6 to 6
- arriving: bfloat16 [8, 2, 4, 21, 21, 384], P('sec', None, 'img'), may hold values from -6 to 6
- head_adjoint: bfloat16 [3, 2, 4, 21, 21, 384], P(None, None, 'img'), may hold values from -6 to 6
- plan: int32 [8, 4], P('sec'), may hold values from 0 to 3, each once within a row
- depth_five: bfloat16 [8, 25, 384], P('sec'), may hold values from -1.25 to 1.25
- depth_three: bfloat16 [8, 9, 384], P('sec'), may hold values from -2 to 2
- point_five: bfloat16 [8, 384, 384], P('sec'), may hold values from -0.3125 to 0.3125
- point_three: bfloat16 [8, 384, 384], P('sec'), may hold values from -0.3125 to 0.3125
Outputs:
- outgoing: bfloat16 [8, 2, 4, 21, 21, 384], P('sec', None, 'img')
- grad_point_five: float32 [8, 384, 384], P('sec', 'img')
- grad_depth_five: float32 [8, 384, 25], P('sec', 'img')
- grad_point_three: float32 [8, 384, 384], P('sec', 'img')
- grad_depth_three: float32 [8, 384, 9], P('sec', 'img')
The draws below stay inside these ranges and needn't reach their ends.
Inputs may be any that keep to these rules, and one draw needn't show every extreme that they name: `plan`: each row is a permutation of the stash slots.
All inputs are finite; a program needn't handle non-finite values.
Results may differ from the reference program's by a relative error of at most 0.012.
Values may be sent and summed in bfloat16 or wider, within the bound.
A program may use at most 128 MiB of HBM per device.

```python
import jax
import jax.numpy as jnp
from jax import lax

C = 384
HGT = 21
WID = 21
KFIVE = 5
KTHREE = 3
STEPS = 4
IMAGES = 4
CELLS = 8


def block_scale(own_key, dims, pieces, low, high):
    level, own = 1.0, jax.random.fold_in(own_key, 6)
    for dim, blocks in pieces:
        steps = jnp.exp(jax.random.uniform(jax.random.fold_in(own, dim), (blocks,), jnp.float32, low / len(pieces), high / len(pieces)))
        level = level * jnp.repeat(steps, dims[dim] // blocks).reshape([-1 if axis == dim else 1 for axis in range(len(dims))])
    return level


def bell_draw(rng, shape, scale, reach, split=(), dtype=jnp.bfloat16):
    drawn = scale * jax.random.normal(rng, shape, jnp.float32)
    if split:
        drawn = drawn * block_scale(rng, shape, split, -0.22, 0.18)
    return jnp.clip(drawn, -reach, reach).astype(dtype)


def setup_inputs(seed: int = 0) -> dict:
    keys = jax.random.split(jax.random.key(seed), 10)
    return {
        "saved_last": bell_draw(keys[0], (CELLS, STEPS, IMAGES, HGT, WID, C), 1.0, 6.0, ((0, 8), (2, 4))),
        "saved_older": bell_draw(keys[1], (CELLS, STEPS, IMAGES, HGT, WID, C), 1.0, 6.0, ((0, 8), (2, 4))),
        "arriving": bell_draw(keys[2], (CELLS, 2, IMAGES, HGT, WID, C), 1.0, 6.0, ((0, 8), (2, 4))),
        "head_adjoint": bell_draw(keys[3], (STEPS - 1, 2, IMAGES, HGT, WID, C), 1.0, 6.0, ((2, 4),)),
        "plan": jax.vmap(lambda own: jax.random.permutation(own, STEPS))(jax.random.split(keys[4], CELLS)).reshape((CELLS, STEPS)).astype(jnp.int32),
        "depth_five": bell_draw(keys[5], (CELLS, KFIVE * KFIVE, C), (KFIVE * KFIVE) ** -0.5, 1.25, ((0, 8),)),
        "depth_three": bell_draw(keys[6], (CELLS, KTHREE * KTHREE, C), (KTHREE * KTHREE) ** -0.5, 2.0, ((0, 8),)),
        "point_five": bell_draw(keys[7], (CELLS, C, C), C ** -0.5, 0.3125, ((0, 8),)),
        "point_three": bell_draw(keys[8], (CELLS, C, C), C ** -0.5, 0.3125, ((0, 8),)),
    }


def depth_apply(active, taps, kernel):
    radius = kernel // 2
    height, breadth = active.shape[1], active.shape[2]
    padded = jnp.pad(active, ((0, 0), (radius, radius), (radius, radius), (0, 0)))
    summed = jnp.zeros(active.shape, jnp.float32)
    for row_tap in range(kernel):
        for col_tap in range(kernel):
            window = padded[:, row_tap:row_tap + height, col_tap:col_tap + breadth, :].astype(jnp.float32)
            summed = summed + taps[row_tap * kernel + col_tap].astype(jnp.float32) * window
    return summed


def depth_transpose(back, taps, kernel):
    radius = kernel // 2
    height, breadth = back.shape[1], back.shape[2]
    padded = jnp.pad(back, ((0, 0), (radius, radius), (radius, radius), (0, 0)))
    summed = jnp.zeros(back.shape, jnp.float32)
    for row_tap in range(kernel):
        for col_tap in range(kernel):
            first_row = 2 * radius - row_tap
            first_col = 2 * radius - col_tap
            window = padded[:, first_row:first_row + height, first_col:first_col + breadth, :]
            summed = summed + taps[row_tap * kernel + col_tap].astype(jnp.float32) * window
    return summed


def depth_taps(active, back, kernel):
    radius = kernel // 2
    height, breadth = active.shape[1], active.shape[2]
    padded = jnp.pad(active, ((0, 0), (radius, radius), (radius, radius), (0, 0)))
    columns = []
    for row_tap in range(kernel):
        for col_tap in range(kernel):
            window = padded[:, row_tap:row_tap + height, col_tap:col_tap + breadth, :].astype(jnp.float32)
            columns.append(jnp.sum(window * back, axis=(0, 1, 2)))
    return jnp.stack(columns, 0)


def cell_backward(last_in, older_in, grad_out, grad_pass, taps_five, taps_three, weight_five, weight_three):
    channels = last_in.shape[3]
    pixels = last_in.shape[0] * last_in.shape[1] * last_in.shape[2]
    factor = 1.0 / (last_in.shape[1] * last_in.shape[2])
    active_last = jax.nn.relu(last_in)
    active_older = jax.nn.relu(older_in)
    mixed_five = depth_apply(active_last, taps_five, 5).astype(jnp.bfloat16)
    mixed_three = depth_apply(active_older, taps_three, 3).astype(jnp.bfloat16)
    flat_grad = grad_out.reshape(pixels, channels)
    back_five = jnp.dot(flat_grad, weight_five.T, preferred_element_type=jnp.float32).reshape(last_in.shape)
    back_three = jnp.dot(flat_grad, weight_three.T, preferred_element_type=jnp.float32).reshape(last_in.shape)
    through_five = depth_transpose(back_five, taps_five, 5)
    grad_last = (grad_pass.astype(jnp.float32) + grad_out.astype(jnp.float32)
                 + jnp.where(last_in > 0, through_five, 0.0)).astype(jnp.bfloat16)
    grad_older = jnp.where(older_in > 0, depth_transpose(back_three, taps_three, 3), 0.0).astype(jnp.bfloat16)
    point_grad_five = jnp.dot(mixed_five.reshape(pixels, channels).T, flat_grad, preferred_element_type=jnp.float32)
    point_grad_three = jnp.dot(mixed_three.reshape(pixels, channels).T, flat_grad, preferred_element_type=jnp.float32)
    taps_grad_five = depth_taps(active_last, back_five, 5)
    taps_grad_three = depth_taps(active_older, back_three, 3)
    grads_five = jnp.concatenate([point_grad_five, taps_grad_five.T], 1) * factor
    grads_three = jnp.concatenate([point_grad_three, taps_grad_three.T], 1) * factor
    return grad_last, grad_older, grads_five, grads_three


def reference(saved_last, saved_older, arriving, head_adjoint, plan, depth_five, depth_three, point_five, point_three):
    sections = saved_last.shape[0]
    turns = saved_last.shape[1]
    channels = saved_last.shape[5]
    totals_five = jnp.zeros((sections, channels, channels + 25), jnp.float32)
    totals_three = jnp.zeros((sections, channels, channels + 9), jnp.float32)
    pairs = arriving
    for turn_index in range(turns):
        if turn_index > 0:
            pairs = jnp.concatenate([pairs[1:], head_adjoint[turn_index - 1][None]], 0)

        def one_section(inputs):
            stash_last, stash_older, slot_index, adjoint_pair, taps_five, taps_three, weight_five, weight_three = inputs
            last_in = lax.dynamic_index_in_dim(stash_last, slot_index, 0, keepdims=False)
            older_in = lax.dynamic_index_in_dim(stash_older, slot_index, 0, keepdims=False)
            grad_last, grad_older, grads_five, grads_three = cell_backward(
                last_in, older_in, adjoint_pair[0], adjoint_pair[1], taps_five, taps_three, weight_five, weight_three)
            return jnp.stack([grad_last, grad_older], 0), grads_five, grads_three

        pairs, grads_five, grads_three = lax.map(one_section, (
            saved_last, saved_older, plan[:, turn_index], pairs, depth_five, depth_three, point_five, point_three))
        totals_five = totals_five + grads_five
        totals_three = totals_three + grads_three
    return (pairs, totals_five[:, :, :channels], totals_five[:, :, channels:],
            totals_three[:, :, :channels], totals_three[:, :, channels:])
```

```python
import functools

import jax
import jax.numpy as jnp
from jax import lax
from jax.experimental import pallas as pl
from jax.experimental.pallas import tpu as pltpu
from jax.sharding import PartitionSpec as P

F32 = jnp.float32
BF16 = jnp.bfloat16
LANES = 128
ROWS = 3
MESH = pl.DeviceIdType.MESH


def up(value, unit):
    return -(-value // unit) * unit


def spread(ref, tap, lanes, height):
    return jnp.broadcast_to(ref[tap : tap + 1, lanes], (height, LANES))


def turned(block, shift, height):
    shift = shift % height
    return block if shift == 0 else pltpu.roll(block, shift, 0)


def filtered(source, taps, kernel, first, lanes, breadth, back):
    radius = kernel // 2
    held = [source[first + k, :, lanes] for k in range(ROWS + kernel - 1)]
    totals = [None] * ROWS
    for col_tap in range(kernel):
        parts = [None] * ROWS
        for row_tap in range(kernel):
            tap = spread(taps, row_tap * kernel + col_tap, lanes, breadth)
            for row in range(ROWS):
                at = row + (kernel - 1 - row_tap if back else row_tap)
                term = tap * held[at]
                parts[row] = term if parts[row] is None else parts[row] + term
        shift = col_tap - radius if back else radius - col_tap
        for row in range(ROWS):
            moved = turned(parts[row], shift, breadth)
            totals[row] = moved if totals[row] is None else totals[row] + moved
    return totals


def tap_sums(active, back, sums, kernel, first, lanes, breadth):
    radius = kernel // 2
    held = [active[first + k, :, lanes] for k in range(ROWS + kernel - 1)]
    rows = [back[first + radius + row, :, lanes] for row in range(ROWS)]
    for col_tap in range(kernel):
        moved = [turned(row, col_tap - radius, breadth) for row in rows]
        for row_tap in range(kernel):
            total = None
            for row in range(ROWS):
                term = held[row + row_tap] * moved[row]
                total = term if total is None else total + term
            folded = total[0:8]
            for part in range(8, breadth, 8):
                folded = folded + total[part : part + 8]
            tap = row_tap * kernel + col_tap
            sums[tap, :, lanes] = sums[tap, :, lanes] + folded


def kernel_body(
    sections,
    group,
    kernels,
    plan,
    last,
    older,
    arriving,
    head,
    depth_five,
    depth_three,
    point_five,
    point_three,
    outgoing,
    out_five,
    out_three,
    out_taps,
    inbox,
    outbox,
    active_five,
    active_three,
    back_five,
    back_three,
    grad_wide,
    grad_flat,
    mixed,
    taps_five,
    taps_three,
    total_five,
    total_three,
    sums_five,
    sums_three,
    sums_all,
    give_five,
    give_three,
    take_five,
    take_three,
    local_sem,
    send_sem,
    recv_sem,
    give_sem,
    take_sem,
):
    five, three = kernels
    turns, height, width, channels = last.shape
    breadth = grad_wide.shape[1]
    rows = channels // group
    factor = 1.0 / (height * width)
    blocks = channels // LANES
    groups = height // ROWS
    sec = lax.axis_index("sec")
    img = lax.axis_index("img")
    top = sec == sections - 1
    bottom = sec == 0
    not_top = sec < sections - 1
    not_bottom = sec > 0

    def first_copy(which):
        return pltpu.make_async_copy(arriving.at[which], inbox.at[0, which], local_sem.at[0, which])

    def head_copy(turn, which):
        return pltpu.make_async_copy(
            head.at[turn - 1, which], inbox.at[turn, which], local_sem.at[turn, which]
        )

    for which in range(2):
        first_copy(which).start()

    @pl.when(top)
    def _():
        for turn in range(1, turns):
            for which in range(2):
                head_copy(turn, which).start()

    barrier = pltpu.get_barrier_semaphore()
    for step in range(1, group):
        pl.semaphore_signal(
            barrier,
            inc=1,
            device_id={"sec": sec, "img": lax.rem(img + step, group)},
            device_id_type=MESH,
        )

    @pl.when(not_bottom)
    def _():
        pl.semaphore_signal(
            barrier, inc=1, device_id={"sec": sec - 1, "img": img}, device_id_type=MESH
        )

    @pl.when(not_top)
    def _():
        pl.semaphore_signal(
            barrier, inc=1, device_id={"sec": sec + 1, "img": img}, device_id_type=MESH
        )

    for ref in (active_five, active_three, back_five, back_three, sums_five, sums_three):
        ref[...] = jnp.zeros(ref.shape, ref.dtype)
    for ref in (total_five, total_three, sums_all, grad_wide):
        ref[...] = jnp.zeros(ref.shape, ref.dtype)
    taps_five[...] = depth_five[...].astype(F32)
    taps_three[...] = depth_three[...].astype(F32)

    def prepare(turn):
        slot = plan[0, turn]

        def one(row, carry):
            active_five[row + five // 2, 0:width, :] = jnp.maximum(last[slot, row].astype(F32), 0.0)
            active_three[row + three // 2, 0:width, :] = jnp.maximum(
                older[slot, row].astype(F32), 0.0
            )
            return carry

        lax.fori_loop(0, height, one, 0)

    def hop(turn, which):
        return pltpu.make_async_remote_copy(
            src_ref=outbox.at[turn, which],
            dst_ref=inbox.at[turn + 1, which],
            send_sem=send_sem.at[turn, which],
            recv_sem=recv_sem.at[turn, which],
            device_id={"sec": lax.max(sec - 1, 0), "img": img},
            device_id_type=MESH,
        )

    def arrive(turn, which):
        @pl.when(top)
        def _():
            head_copy(turn, which).wait()

        @pl.when(not_top)
        def _():
            hop(turn - 1, which).wait_recv()

    def spread_grad(turn):
        def one(row, carry):
            grad_wide[row, 0:width, :] = inbox[turn, 0, row].astype(F32)
            return carry

        lax.fori_loop(0, height, one, 0)
        grad_flat[...] = grad_wide[...].reshape(height * breadth, channels).astype(BF16)

    def pull(weights, back, kernel):
        product = lax.dot_general(
            grad_flat[...], weights[...], (((1,), (1,)), ((), ())), preferred_element_type=F32
        )
        back[kernel // 2 : kernel // 2 + height] = product.reshape(height, breadth, channels)

    def each_block(work):
        def one(index, carry):
            lanes = pl.ds(pl.multiple_of((index // groups) * LANES, LANES), LANES)
            work((index % groups) * ROWS, lanes)
            return carry

        lax.fori_loop(0, blocks * groups, one, 0)

    def through_five(turn, target):
        def work(first, lanes):
            outs = filtered(back_five, taps_five, five, first, lanes, breadth, True)
            for row in range(ROWS):
                at = first + row
                kept = jnp.where(active_five[at + five // 2, :, lanes] > 0, outs[row], 0.0)
                extra = inbox[turn, 1, at, :, lanes].astype(F32)
                done = kept[0:width] + grad_wide[at, 0:width, lanes] + extra
                target[at, :, lanes] = done.astype(BF16)

        each_block(work)

    def through_three(target):
        def work(first, lanes):
            outs = filtered(back_three, taps_three, three, first, lanes, breadth, True)
            for row in range(ROWS):
                at = first + row
                kept = jnp.where(active_three[at + three // 2, :, lanes] > 0, outs[row], 0.0)
                target[at, :, lanes] = kept[0:width].astype(BF16)

        each_block(work)

    def weights(active, taps, back, sums, total, kernel):
        def work(first, lanes):
            outs = filtered(active, taps, kernel, first, lanes, breadth, False)
            for row in range(ROWS):
                mixed[first + row, :, lanes] = outs[row]
            tap_sums(active, back, sums, kernel, first, lanes, breadth)

        each_block(work)
        flat = mixed[...].reshape(height * breadth, channels).astype(BF16)
        total[...] += lax.dot_general(
            flat, grad_flat[...], (((0,), (0,)), ((), ())), preferred_element_type=F32
        )

    def weights_five():
        weights(active_five, taps_five, back_five, sums_five, total_five, five)

    def weights_three():
        weights(active_three, taps_three, back_three, sums_three, total_three, three)

    def share(part, step):
        source, target = ((give_five, take_five), (give_three, take_three))[part]
        peer = lax.rem(img + step, group)
        return pltpu.make_async_remote_copy(
            src_ref=source.at[peer],
            dst_ref=target.at[step],
            send_sem=give_sem.at[part, step],
            recv_sem=take_sem.at[part, step],
            device_id={"sec": sec, "img": peer},
            device_id_type=MESH,
        )

    prepare(0)
    callers = group + 1 - bottom.astype(jnp.int32) - top.astype(jnp.int32)
    pl.semaphore_wait(barrier, callers)

    first_copy(0).wait()
    first_copy(1).wait()

    def turn_work(turn, carry):
        spread_grad(turn)
        pull(point_five, back_five, five)

        @pl.when(turn > 0)
        def _():
            arrive(turn, 1)

        through_five(turn, outbox.at[turn, 0])

        @pl.when(not_bottom)
        def _():
            hop(turn, 0).start()

        pull(point_three, back_three, three)
        through_three(outbox.at[turn, 1])

        @pl.when(not_bottom)
        def _():
            hop(turn, 1).start()

        weights_five()
        weights_three()
        prepare(turn + 1)
        arrive(turn + 1, 0)
        return carry

    lax.fori_loop(0, turns - 1, turn_work, 0)

    end = turns - 1
    spread_grad(end)
    pull(point_five, back_five, five)
    pull(point_three, back_three, three)
    weights_five()
    for peer in range(group):
        give_five[peer] = (total_five[peer * rows : (peer + 1) * rows] * factor).astype(BF16)
    for step in range(1, group):
        share(0, step).start()
    weights_three()
    count_five, count_three = five * five, three * three
    sums_all[0:count_five] = jnp.sum(sums_five[...], axis=1)
    sums_all[count_five : count_five + count_three] = jnp.sum(sums_three[...], axis=1)
    flipped = sums_all[...].T * factor
    for peer in range(group):
        part = slice(peer * rows, (peer + 1) * rows)
        give_three[peer, :, 0:channels] = (total_three[part] * factor).astype(BF16)
        give_three[peer, :, channels:] = flipped[part].astype(BF16)
    for step in range(1, group):
        share(1, step).start()
    arrive(end, 1)
    through_five(end, outgoing.at[0])
    through_three(outgoing.at[1])

    gathered_five = give_five[img].astype(F32)
    for step in range(1, group):
        share(0, step).wait_recv()
        gathered_five = gathered_five + take_five[step].astype(F32)
    out_five[...] = gathered_five
    gathered = give_three[img].astype(F32)
    for step in range(1, group):
        share(1, step).wait_recv()
        gathered = gathered + take_three[step].astype(F32)
    out_three[...] = gathered[:, 0:channels]
    out_taps[...] = gathered[:, channels:]
    for part in range(2):
        for step in range(1, group):
            share(part, step).wait_send()

    @pl.when(not_bottom)
    def _():
        for turn in range(turns - 1):
            for which in range(2):
                hop(turn, which).wait_send()


def local(
    sections,
    group,
    saved_last,
    saved_older,
    arriving,
    head_adjoint,
    plan,
    depth_five,
    depth_three,
    point_five,
    point_three,
):
    turns, _, height, width, channels = saved_last.shape[1:]
    count_five, count_three = depth_five.shape[1], depth_three.shape[1]
    five, three = round(count_five**0.5), round(count_three**0.5)
    breadth = up(width + five // 2, 8)
    rows = channels // group
    vmem = pl.BlockSpec(memory_space=pltpu.VMEM)
    smem = pl.BlockSpec(memory_space=pltpu.SMEM)
    outside = pl.BlockSpec(memory_space=pl.ANY)
    body = functools.partial(kernel_body, sections, group, (five, three))
    outgoing, grad_five, grad_three, grad_taps = pl.pallas_call(
        body,
        out_shape=(
            jax.ShapeDtypeStruct((2, height, width, channels), BF16),
            jax.ShapeDtypeStruct((rows, channels), F32),
            jax.ShapeDtypeStruct((rows, channels), F32),
            jax.ShapeDtypeStruct((rows, LANES), F32),
        ),
        in_specs=[smem, vmem, vmem, outside, outside, vmem, vmem, vmem, vmem],
        out_specs=(vmem, vmem, vmem, vmem),
        scratch_shapes=[
            pltpu.VMEM((turns, 2, height, width, channels), BF16),
            pltpu.VMEM((turns - 1, 2, height, width, channels), BF16),
            pltpu.VMEM((height + five - 1, breadth, channels), F32),
            pltpu.VMEM((height + three - 1, breadth, channels), F32),
            pltpu.VMEM((height + five - 1, breadth, channels), F32),
            pltpu.VMEM((height + three - 1, breadth, channels), F32),
            pltpu.VMEM((height, breadth, channels), F32),
            pltpu.VMEM((height * breadth, channels), BF16),
            pltpu.VMEM((height, breadth, channels), F32),
            pltpu.VMEM((count_five, channels), F32),
            pltpu.VMEM((count_three, channels), F32),
            pltpu.VMEM((channels, channels), F32),
            pltpu.VMEM((channels, channels), F32),
            pltpu.VMEM((count_five, 8, channels), F32),
            pltpu.VMEM((count_three, 8, channels), F32),
            pltpu.VMEM((LANES, channels), F32),
            pltpu.VMEM((group, rows, channels), BF16),
            pltpu.VMEM((group, rows, channels + LANES), BF16),
            pltpu.VMEM((group, rows, channels), BF16),
            pltpu.VMEM((group, rows, channels + LANES), BF16),
            pltpu.SemaphoreType.DMA((turns, 2)),
            pltpu.SemaphoreType.DMA((turns - 1, 2)),
            pltpu.SemaphoreType.DMA((turns - 1, 2)),
            pltpu.SemaphoreType.DMA((2, group)),
            pltpu.SemaphoreType.DMA((2, group)),
        ],
        compiler_params=pltpu.CompilerParams(collective_id=0, has_side_effects=True),
    )(
        plan,
        saved_last.reshape(turns, height, width, channels),
        saved_older.reshape(turns, height, width, channels),
        arriving.reshape(2, height, width, channels),
        head_adjoint.reshape(turns - 1, 2, height, width, channels),
        depth_five[0],
        depth_three[0],
        point_five[0],
        point_three[0],
    )
    return (
        outgoing.reshape(1, 2, 1, height, width, channels),
        grad_five[None],
        grad_taps[None, :, :count_five],
        grad_three[None],
        grad_taps[None, :, count_five : count_five + count_three],
    )


def solution(mesh):
    placed = (
        P("sec", None, "img", None, None, None),
        P("sec", None, "img", None, None, None),
        P("sec", None, "img", None, None, None),
        P(None, None, "img", None, None, None),
        P("sec", None),
        P("sec", None, None),
        P("sec", None, None),
        P("sec", None, None),
        P("sec", None, None),
    )
    return jax.shard_map(
        functools.partial(local, mesh.shape["sec"], mesh.shape["img"]),
        mesh=mesh,
        in_specs=placed,
        out_specs=(
            P("sec", None, "img", None, None, None),
            P("sec", "img", None),
            P("sec", "img", None),
            P("sec", "img", None),
            P("sec", "img", None),
        ),
        check_vma=False,
    )
```

```python
import functools

import jax
import jax.numpy as jnp
from jax import lax
from jax.experimental import pallas as pl
from jax.experimental.pallas import tpu as pltpu
from jax.sharding import PartitionSpec as P

F32 = jnp.float32
BF16 = jnp.bfloat16
LANES = 128
WIDE = 256
MESH = pl.DeviceIdType.MESH


def up(value, unit):
    return -(-value // unit) * unit


def turned(block, shift):
    shift = shift % block.shape[0]
    return block if shift == 0 else pltpu.roll(block, shift, 0)


def rows_at(even, odd, pair, offset, lanes):
    if offset % 2 == 0:
        block = even[pair + offset // 2 + 1, :, lanes]
    else:
        block = odd[pair + (offset + 1) // 2, :, lanes]
    return block.reshape(-1, 8, WIDE)


def filtered(even, odd, taps, kernel, pair, lanes, back):
    radius = kernel // 2
    held = [rows_at(even, odd, pair, k - radius, lanes) for k in range(kernel)]
    total = None
    for col_tap in range(kernel):
        part = None
        for row_tap in range(kernel):
            at = kernel - 1 - row_tap if back else row_tap
            term = taps[row_tap * kernel + col_tap, :, lanes][None] * held[at]
            part = term if part is None else part + term
        wide = part.astype(F32).reshape(-1, WIDE)
        moved = turned(wide, col_tap - radius if back else radius - col_tap)
        total = moved if total is None else total + moved
    return total


def tap_sums(even, odd, back, sums, kernel, pair, lanes):
    radius = kernel // 2
    held = [rows_at(even, odd, pair, k - radius, lanes) for k in range(kernel)]
    wide = back[pair + 1, :, lanes].astype(F32)
    for col_tap in range(kernel):
        moved = turned(wide, col_tap - radius).astype(BF16).reshape(-1, 8, WIDE)
        for row_tap in range(kernel):
            term = held[row_tap] * moved
            folded = term[0]
            for part in range(1, term.shape[0]):
                folded = folded + term[part]
            tap = row_tap * kernel + col_tap
            sums[tap, :, lanes] = sums[tap, :, lanes] + folded.astype(F32)


def kernel_body(
    sections,
    group,
    kernels,
    plan,
    last,
    older,
    arriving,
    head,
    depth_five,
    depth_three,
    point_five,
    point_three,
    outgoing,
    out_five,
    out_three,
    out_taps,
    inbox,
    outbox,
    stage,
    even_last,
    odd_last,
    even_older,
    odd_older,
    even_five,
    odd_five,
    even_three,
    odd_three,
    grad_wide,
    grad_flat,
    mixed,
    taps_five,
    taps_three,
    total_five,
    total_three,
    sums_five,
    sums_three,
    sums_all,
    give_five,
    give_three,
    take_five,
    take_three,
    local_sem,
    send_sem,
    recv_sem,
    give_sem,
    take_sem,
):
    five, three = kernels
    turns, height, width, channels = last.shape
    breadth = grad_wide.shape[1]
    rows = channels // group
    factor = 1.0 / (height * width)
    blocks = 2 * channels // WIDE
    columns = channels // LANES
    pairs = grad_wide.shape[0] // 2
    sec = lax.axis_index("sec")
    img = lax.axis_index("img")
    top = sec == sections - 1
    bottom = sec == 0
    not_top = sec < sections - 1
    not_bottom = sec > 0

    def first_copy(which):
        return pltpu.make_async_copy(arriving.at[which], inbox.at[0, which, pl.ds(0, height)], local_sem.at[0, which])

    def head_copy(turn, which):
        return pltpu.make_async_copy(
            head.at[turn - 1, which], inbox.at[turn, which, pl.ds(0, height)], local_sem.at[turn, which]
        )

    for which in range(2):
        first_copy(which).start()

    @pl.when(top)
    def _():
        for turn in range(1, turns):
            for which in range(2):
                head_copy(turn, which).start()

    barrier = pltpu.get_barrier_semaphore()
    for step in range(1, group):
        pl.semaphore_signal(
            barrier,
            inc=1,
            device_id={"sec": sec, "img": lax.rem(img + step, group)},
            device_id_type=MESH,
        )

    @pl.when(not_bottom)
    def _():
        pl.semaphore_signal(
            barrier, inc=1, device_id={"sec": sec - 1, "img": img}, device_id_type=MESH
        )

    @pl.when(not_top)
    def _():
        pl.semaphore_signal(
            barrier, inc=1, device_id={"sec": sec + 1, "img": img}, device_id_type=MESH
        )

    for ref in (sums_five, sums_three, total_five, total_three, sums_all):
        ref[...] = jnp.zeros(ref.shape, ref.dtype)
    edge_even = jnp.zeros(even_five.shape[1:], BF16)
    for ref in (even_last, even_older, even_five, even_three):
        ref[0] = edge_even
        ref[pairs + 1] = edge_even
    for ref in (odd_last, odd_older, odd_five, odd_three):
        ref[pairs] = edge_even
    for row in range(stage.shape[0]):
        stage[row, breadth - 8 : breadth] = jnp.zeros((8, channels), F32)
    for row in range(grad_wide.shape[0]):
        grad_wide[row, breadth - 8 : breadth] = jnp.zeros((8, channels), F32)
    for row in (0, *range(height + 1, stage.shape[0])):
        stage[row] = jnp.zeros((breadth, channels), F32)
    for row in range(height, grad_wide.shape[0]):
        grad_wide[row] = jnp.zeros((breadth, channels), F32)
    for wide, packed in ((depth_five, taps_five), (depth_three, taps_three)):
        for tap in range(packed.shape[0]):
            value = jnp.broadcast_to(wide[tap : tap + 1].astype(F32), (8, channels))
            packed[tap] = jnp.concatenate([value, value], 1).astype(BF16)

    def prepare(turn):
        slot = plan[0, turn]
        for saved, even, odd in ((last, even_last, odd_last), (older, even_older, odd_older)):

            def one(row, carry):
                stage[row + 1, 0:width, :] = jnp.maximum(saved[slot, row].astype(F32), 0.0)
                return carry

            lax.fori_loop(0, height, one, 0, unroll=3)

            def two(pair, carry):
                rows = [stage[2 * pair + k] for k in range(3)]
                odd[pair] = jnp.concatenate(rows[0:2], 1).astype(BF16)
                even[pair + 1] = jnp.concatenate(rows[1:3], 1).astype(BF16)
                return carry

            lax.fori_loop(0, pairs, two, 0)

    def hop(turn, which):
        return pltpu.make_async_remote_copy(
            src_ref=outbox.at[turn, which, pl.ds(0, height)],
            dst_ref=inbox.at[turn + 1, which, pl.ds(0, height)],
            send_sem=send_sem.at[turn, which],
            recv_sem=recv_sem.at[turn, which],
            device_id={"sec": lax.max(sec - 1, 0), "img": img},
            device_id_type=MESH,
        )

    def arrive(turn, which):
        @pl.when(top)
        def _():
            head_copy(turn, which).wait()

        @pl.when(not_top)
        def _():
            hop(turn - 1, which).wait_recv()

    def spread_grad(turn):
        def one(row, carry):
            grad_wide[row, 0:width, :] = inbox[turn, 0, row].astype(F32)
            return carry

        lax.fori_loop(0, height, one, 0, unroll=3)
        grad_flat[...] = grad_wide[0:height].reshape(-1, channels).astype(BF16)

    def pull(weights, even, odd):
        product = lax.dot_general(
            grad_flat[...], weights[...], (((1,), (1,)), ((), ())), preferred_element_type=F32
        )
        zeros = jnp.zeros((breadth, channels), F32)

        def line(row):
            inside = 0 <= row < height
            return product[row * breadth : (row + 1) * breadth] if inside else zeros

        for pair in range(pairs):
            even[pair + 1] = jnp.concatenate([line(2 * pair), line(2 * pair + 1)], 1).astype(BF16)
            odd[pair] = jnp.concatenate([line(2 * pair - 1), line(2 * pair)], 1).astype(BF16)

    def parts(pair, block):
        for part in range(WIDE // LANES):
            at = block * (WIDE // LANES) + part
            lanes = slice((at % columns) * LANES, (at % columns + 1) * LANES)
            yield 2 * pair + at // columns, lanes, slice(part * LANES, (part + 1) * LANES)

    def each_block(work):
        def one(pair, carry):
            for block in range(blocks):
                work(pair, block, slice(block * WIDE, (block + 1) * WIDE))
            return carry

        lax.fori_loop(0, pairs, one, 0)

    def through_five(turn, target):
        def work(pair, block, wide):
            out = filtered(even_five, odd_five, taps_five, five, pair, wide, True)
            kept = jnp.where(even_last[pair + 1, :, wide].astype(F32) > 0, out, 0.0)
            for at, lanes, cut in parts(pair, block):
                extra = inbox[turn, 1, at, :, lanes].astype(F32)
                done = kept[0:width, cut] + grad_wide[at, 0:width, lanes] + extra
                target[at, :, lanes] = done.astype(BF16)

        each_block(work)

    def through_three(target):
        def work(pair, block, wide):
            out = filtered(even_three, odd_three, taps_three, three, pair, wide, True)
            kept = jnp.where(even_older[pair + 1, :, wide].astype(F32) > 0, out, 0.0)
            for at, lanes, cut in parts(pair, block):
                target[at, :, lanes] = kept[0:width, cut].astype(BF16)

        each_block(work)

    def weights(even, odd, taps, back, sums, total, kernel):
        def work(pair, block, wide):
            out = filtered(even, odd, taps, kernel, pair, wide, False)
            for at, lanes, cut in parts(pair, block):
                mixed[at, :, lanes] = out[:, cut]
            tap_sums(even, odd, back, sums, kernel, pair, wide)

        each_block(work)
        flat = mixed[0:height].reshape(-1, channels).astype(BF16)
        total[...] += lax.dot_general(
            flat, grad_flat[...], (((0,), (0,)), ((), ())), preferred_element_type=F32
        )

    def weights_five():
        weights(even_last, odd_last, taps_five, even_five, sums_five, total_five, five)

    def weights_three():
        weights(even_older, odd_older, taps_three, even_three, sums_three, total_three, three)

    def share(part, step):
        source, target = ((give_five, take_five), (give_three, take_three))[part]
        peer = lax.rem(img + step, group)
        return pltpu.make_async_remote_copy(
            src_ref=source.at[peer],
            dst_ref=target.at[step],
            send_sem=give_sem.at[part, step],
            recv_sem=take_sem.at[part, step],
            device_id={"sec": sec, "img": peer},
            device_id_type=MESH,
        )

    prepare(0)
    callers = group + 1 - bottom.astype(jnp.int32) - top.astype(jnp.int32)
    pl.semaphore_wait(barrier, callers)

    first_copy(0).wait()
    first_copy(1).wait()

    def turn_work(turn, carry):
        spread_grad(turn)
        pull(point_five, even_five, odd_five)

        @pl.when(turn > 0)
        def _():
            arrive(turn, 1)

        through_five(turn, outbox.at[turn, 0])

        @pl.when(not_bottom)
        def _():
            hop(turn, 0).start()

        pull(point_three, even_three, odd_three)
        through_three(outbox.at[turn, 1])

        @pl.when(not_bottom)
        def _():
            hop(turn, 1).start()

        weights_five()
        weights_three()
        prepare(turn + 1)
        arrive(turn + 1, 0)
        return carry

    lax.fori_loop(0, turns - 1, turn_work, 0)

    end = turns - 1
    spread_grad(end)
    pull(point_five, even_five, odd_five)
    pull(point_three, even_three, odd_three)
    weights_five()
    for peer in range(group):
        give_five[peer] = (total_five[peer * rows : (peer + 1) * rows] * factor).astype(BF16)
    for step in range(1, group):
        share(0, step).start()
    weights_three()
    count_five, count_three = five * five, three * three
    for sums, start, count in ((sums_five, 0, count_five), (sums_three, count_five, count_three)):
        folded = jnp.sum(sums[...], axis=1)
        sums_all[start : start + count] = folded[:, 0:channels] + folded[:, channels:]
    flipped = sums_all[...].T * factor
    for peer in range(group):
        part = slice(peer * rows, (peer + 1) * rows)
        give_three[peer, :, 0:channels] = (total_three[part] * factor).astype(BF16)
        give_three[peer, :, channels:] = flipped[part].astype(BF16)
    for step in range(1, group):
        share(1, step).start()
    arrive(end, 1)
    through_five(end, outgoing.at[0])
    through_three(outgoing.at[1])

    gathered_five = give_five[img].astype(F32)
    for step in range(1, group):
        share(0, step).wait_recv()
        gathered_five = gathered_five + take_five[step].astype(F32)
    out_five[...] = gathered_five
    gathered = give_three[img].astype(F32)
    for step in range(1, group):
        share(1, step).wait_recv()
        gathered = gathered + take_three[step].astype(F32)
    out_three[...] = gathered[:, 0:channels]
    out_taps[...] = gathered[:, channels:]
    for part in range(2):
        for step in range(1, group):
            share(part, step).wait_send()

    @pl.when(not_bottom)
    def _():
        for turn in range(turns - 1):
            for which in range(2):
                hop(turn, which).wait_send()


def local(
    sections,
    group,
    saved_last,
    saved_older,
    arriving,
    head_adjoint,
    plan,
    depth_five,
    depth_three,
    point_five,
    point_three,
):
    turns, _, height, width, channels = saved_last.shape[1:]
    count_five, count_three = depth_five.shape[1], depth_three.shape[1]
    five, three = round(count_five**0.5), round(count_three**0.5)
    breadth = up(width + five // 2, 8)
    pairs = up(height, 2) // 2
    even = pltpu.VMEM((pairs + 2, breadth, 2 * channels), BF16)
    odd = pltpu.VMEM((pairs + 1, breadth, 2 * channels), BF16)
    rows = channels // group
    vmem = pl.BlockSpec(memory_space=pltpu.VMEM)
    smem = pl.BlockSpec(memory_space=pltpu.SMEM)
    outside = pl.BlockSpec(memory_space=pl.ANY)
    body = functools.partial(kernel_body, sections, group, (five, three))
    outgoing, grad_five, grad_three, grad_taps = pl.pallas_call(
        body,
        out_shape=(
            jax.ShapeDtypeStruct((2, 2 * pairs, width, channels), BF16),
            jax.ShapeDtypeStruct((rows, channels), F32),
            jax.ShapeDtypeStruct((rows, channels), F32),
            jax.ShapeDtypeStruct((rows, LANES), F32),
        ),
        in_specs=[smem, vmem, vmem, outside, outside, vmem, vmem, vmem, vmem],
        out_specs=(vmem, vmem, vmem, vmem),
        scratch_shapes=[
            pltpu.VMEM((turns, 2, 2 * pairs, width, channels), BF16),
            pltpu.VMEM((turns - 1, 2, 2 * pairs, width, channels), BF16),
            pltpu.VMEM((2 * pairs + 2, breadth, channels), F32),
            *([even, odd] * 4),
            pltpu.VMEM((2 * pairs, breadth, channels), F32),
            pltpu.VMEM((height * breadth, channels), BF16),
            pltpu.VMEM((2 * pairs, breadth, channels), F32),
            pltpu.VMEM((count_five, 8, 2 * channels), BF16),
            pltpu.VMEM((count_three, 8, 2 * channels), BF16),
            pltpu.VMEM((channels, channels), F32),
            pltpu.VMEM((channels, channels), F32),
            pltpu.VMEM((count_five, 8, 2 * channels), F32),
            pltpu.VMEM((count_three, 8, 2 * channels), F32),
            pltpu.VMEM((LANES, channels), F32),
            pltpu.VMEM((group, rows, channels), BF16),
            pltpu.VMEM((group, rows, channels + LANES), BF16),
            pltpu.VMEM((group, rows, channels), BF16),
            pltpu.VMEM((group, rows, channels + LANES), BF16),
            pltpu.SemaphoreType.DMA((turns, 2)),
            pltpu.SemaphoreType.DMA((turns - 1, 2)),
            pltpu.SemaphoreType.DMA((turns - 1, 2)),
            pltpu.SemaphoreType.DMA((2, group)),
            pltpu.SemaphoreType.DMA((2, group)),
        ],
        compiler_params=pltpu.CompilerParams(collective_id=0, has_side_effects=True),
    )(
        plan,
        saved_last.reshape(turns, height, width, channels),
        saved_older.reshape(turns, height, width, channels),
        arriving.reshape(2, height, width, channels),
        head_adjoint.reshape(turns - 1, 2, height, width, channels),
        depth_five[0],
        depth_three[0],
        point_five[0],
        point_three[0],
    )
    return (
        outgoing[:, :height].reshape(1, 2, 1, height, width, channels),
        grad_five[None],
        grad_taps[None, :, :count_five],
        grad_three[None],
        grad_taps[None, :, count_five : count_five + count_three],
    )


def solution(mesh):
    placed = (
        P("sec", None, "img", None, None, None),
        P("sec", None, "img", None, None, None),
        P("sec", None, "img", None, None, None),
        P(None, None, "img", None, None, None),
        P("sec", None),
        P("sec", None, None),
        P("sec", None, None),
        P("sec", None, None),
        P("sec", None, None),
    )
    return jax.shard_map(
        functools.partial(local, mesh.shape["sec"], mesh.shape["img"]),
        mesh=mesh,
        in_specs=placed,
        out_specs=(
            P("sec", None, "img", None, None, None),
            P("sec", "img", None),
            P("sec", "img", None),
            P("sec", "img", None),
            P("sec", "img", None),
        ),
        check_vma=False,
    )
```

```python
import functools

import jax
import jax.numpy as jnp
from jax import lax
from jax.experimental import pallas as pl
from jax.experimental.pallas import tpu as pltpu
from jax.sharding import PartitionSpec as P

F32 = jnp.float32
BF16 = jnp.bfloat16
LANES = 128
WIDE = 256
MESH = pl.DeviceIdType.MESH


def up(value, unit):
    return -(-value // unit) * unit


def turned(block, shift):
    shift = shift % block.shape[0]
    return block if shift == 0 else pltpu.roll(block, shift, 0)


def rows_at(even, odd, pair, offset, lanes):
    if offset % 2 == 0:
        block = even[pair + offset // 2 + 1, :, lanes]
    else:
        block = odd[pair + (offset + 1) // 2, :, lanes]
    return block.reshape(-1, 8, WIDE)


def filtered(even, odd, taps, kernel, pair, lanes, back):
    radius = kernel // 2
    held = [rows_at(even, odd, pair, k - radius, lanes) for k in range(kernel)]
    total = None
    for col_tap in range(kernel):
        part = None
        for row_tap in range(kernel):
            at = kernel - 1 - row_tap if back else row_tap
            term = taps[row_tap * kernel + col_tap, :, lanes][None] * held[at]
            part = term if part is None else part + term
        wide = part.astype(F32).reshape(-1, WIDE)
        moved = turned(wide, col_tap - radius if back else radius - col_tap)
        total = moved if total is None else total + moved
    return total


def tap_sums(even, odd, back, sums, kernel, pair, lanes):
    radius = kernel // 2
    held = [rows_at(even, odd, pair, k - radius, lanes) for k in range(kernel)]
    wide = back[pair + 1, :, lanes].astype(F32)
    for col_tap in range(kernel):
        moved = turned(wide, col_tap - radius).astype(BF16).reshape(-1, 8, WIDE)
        for row_tap in range(kernel):
            term = held[row_tap] * moved
            folded = term[0]
            for part in range(1, term.shape[0]):
                folded = folded + term[part]
            tap = row_tap * kernel + col_tap
            sums[tap, :, lanes] = sums[tap, :, lanes] + folded.astype(F32)


def kernel_body(
    sections,
    group,
    kernels,
    plan,
    last,
    older,
    arriving_last,
    arriving_older,
    head_last,
    head_older,
    depth_five,
    depth_three,
    point_five,
    point_three,
    outgoing,
    out_five,
    out_three,
    out_taps_five,
    out_taps_three,
    inbox,
    outbox,
    stage,
    even_last,
    odd_last,
    even_older,
    odd_older,
    even_five,
    odd_five,
    even_three,
    odd_three,
    grad_wide,
    grad_flat,
    mixed_five,
    mixed_three,
    taps_five,
    taps_three,
    total_five,
    total_three,
    sums_five,
    sums_three,
    sums_all,
    give_five,
    give_three,
    give_taps,
    take_five,
    take_three,
    take_taps,
    local_sem,
    send_sem,
    recv_sem,
    give_sem,
    take_sem,
):
    five, three = kernels
    turns, height, width, channels = last.shape
    breadth = grad_wide.shape[1]
    rows = channels // group
    factor = 1.0 / (height * width)
    blocks = 2 * channels // WIDE
    columns = channels // LANES
    pairs = grad_wide.shape[0] // 2
    sec = lax.axis_index("sec")
    img = lax.axis_index("img")
    top = sec == sections - 1
    bottom = sec == 0
    not_top = sec < sections - 1
    not_bottom = sec > 0

    def first_copy(which):
        source = (arriving_last, arriving_older)[which]
        target = inbox.at[0, which, pl.ds(0, height)]
        return pltpu.make_async_copy(source, target, local_sem.at[0, which])

    def head_copy(turn, which):
        source = (head_last, head_older)[which].at[turn - 1]
        target = inbox.at[turn, which, pl.ds(0, height)]
        return pltpu.make_async_copy(source, target, local_sem.at[turn, which])

    for which in range(2):
        first_copy(which).start()

    @pl.when(top)
    def _():
        for turn in range(1, turns):
            for which in range(2):
                head_copy(turn, which).start()

    barrier = pltpu.get_barrier_semaphore()
    for step in range(1, group):
        pl.semaphore_signal(
            barrier,
            inc=1,
            device_id={"sec": sec, "img": lax.rem(img + step, group)},
            device_id_type=MESH,
        )

    @pl.when(not_bottom)
    def _():
        pl.semaphore_signal(
            barrier, inc=1, device_id={"sec": sec - 1, "img": img}, device_id_type=MESH
        )

    @pl.when(not_top)
    def _():
        pl.semaphore_signal(
            barrier, inc=1, device_id={"sec": sec + 1, "img": img}, device_id_type=MESH
        )

    for ref in (sums_five, sums_three, total_five, total_three, sums_all):
        ref[...] = jnp.zeros(ref.shape, ref.dtype)
    edge_even = jnp.zeros(even_five.shape[1:], BF16)
    for ref in (even_last, even_older, even_five, even_three):
        ref[0] = edge_even
        ref[pairs + 1] = edge_even
    for ref in (odd_last, odd_older, odd_five, odd_three):
        ref[pairs] = edge_even
    for row in range(stage.shape[0]):
        stage[row, breadth - 8 : breadth] = jnp.zeros((8, channels), F32)
    for row in range(grad_wide.shape[0]):
        grad_wide[row, breadth - 8 : breadth] = jnp.zeros((8, channels), F32)
    for row in (0, *range(height + 1, stage.shape[0])):
        stage[row] = jnp.zeros((breadth, channels), F32)
    for row in range(height, grad_wide.shape[0]):
        grad_wide[row] = jnp.zeros((breadth, channels), F32)
    for wide, packed in ((depth_five, taps_five), (depth_three, taps_three)):
        for tap in range(packed.shape[0]):
            value = jnp.broadcast_to(wide[tap : tap + 1].astype(F32), (8, channels))
            packed[tap] = jnp.concatenate([value, value], 1).astype(BF16)

    def prepare(turn):
        slot = plan[0, turn]
        for saved, even, odd in ((last, even_last, odd_last), (older, even_older, odd_older)):

            def one(row, carry):
                stage[row + 1, 0:width, :] = jnp.maximum(saved[slot, row].astype(F32), 0.0)
                return carry

            lax.fori_loop(0, height, one, 0, unroll=3)

            def two(pair, carry):
                rows = [stage[2 * pair + k] for k in range(3)]
                odd[pair] = jnp.concatenate(rows[0:2], 1).astype(BF16)
                even[pair + 1] = jnp.concatenate(rows[1:3], 1).astype(BF16)
                return carry

            lax.fori_loop(0, pairs, two, 0)

    def hop(turn, which):
        return pltpu.make_async_remote_copy(
            src_ref=outbox.at[turn, which, pl.ds(0, height)],
            dst_ref=inbox.at[turn + 1, which, pl.ds(0, height)],
            send_sem=send_sem.at[turn, which],
            recv_sem=recv_sem.at[turn, which],
            device_id={"sec": lax.max(sec - 1, 0), "img": img},
            device_id_type=MESH,
        )

    def arrive(turn, which):
        @pl.when(top)
        def _():
            head_copy(turn, which).wait()

        @pl.when(not_top)
        def _():
            hop(turn - 1, which).wait_recv()

    def spread_grad(turn):
        def one(row, carry):
            grad_wide[row, 0:width, :] = inbox[turn, 0, row].astype(F32)
            return carry

        lax.fori_loop(0, height, one, 0, unroll=3)
        grad_flat[...] = grad_wide[0:height].reshape(-1, channels).astype(BF16)

    def pull(weights, even, odd):
        product = lax.dot_general(
            grad_flat[...], weights[...], (((1,), (1,)), ((), ())), preferred_element_type=F32
        )
        zeros = jnp.zeros((breadth, channels), F32)

        def line(row):
            inside = 0 <= row < height
            return product[row * breadth : (row + 1) * breadth] if inside else zeros

        for pair in range(pairs):
            even[pair + 1] = jnp.concatenate([line(2 * pair), line(2 * pair + 1)], 1).astype(BF16)
            odd[pair] = jnp.concatenate([line(2 * pair - 1), line(2 * pair)], 1).astype(BF16)

    def parts(pair, block):
        for part in range(WIDE // LANES):
            at = block * (WIDE // LANES) + part
            lanes = slice((at % columns) * LANES, (at % columns + 1) * LANES)
            yield 2 * pair + at // columns, lanes, slice(part * LANES, (part + 1) * LANES)

    def each_block(work):
        def one(pair, carry):
            for block in range(blocks):
                work(pair, block, slice(block * WIDE, (block + 1) * WIDE))
            return carry

        lax.fori_loop(0, pairs, one, 0)

    def through_five(turn, target):
        def work(pair, block, wide):
            out = filtered(even_five, odd_five, taps_five, five, pair, wide, True)
            kept = jnp.where(even_last[pair + 1, :, wide].astype(F32) > 0, out, 0.0)
            for at, lanes, cut in parts(pair, block):
                extra = inbox[turn, 1, at, :, lanes].astype(F32)
                done = kept[0:width, cut] + grad_wide[at, 0:width, lanes] + extra
                target[at, :, lanes] = done.astype(BF16)

        each_block(work)

    def through_three(target):
        def work(pair, block, wide):
            out = filtered(even_three, odd_three, taps_three, three, pair, wide, True)
            kept = jnp.where(even_older[pair + 1, :, wide].astype(F32) > 0, out, 0.0)
            for at, lanes, cut in parts(pair, block):
                target[at, :, lanes] = kept[0:width, cut].astype(BF16)

        each_block(work)

    def forward():
        def work(pair, block, wide):
            for even, odd, taps, mixed, kernel in (
                (even_last, odd_last, taps_five, mixed_five, five),
                (even_older, odd_older, taps_three, mixed_three, three),
            ):
                out = filtered(even, odd, taps, kernel, pair, wide, False)
                for at, lanes, cut in parts(pair, block):
                    mixed[at, :, lanes] = out[:, cut]

        each_block(work)

    def add_taps():
        def work(pair, block, wide):
            tap_sums(even_last, odd_last, even_five, sums_five, five, pair, wide)
            tap_sums(even_older, odd_older, even_three, sums_three, three, pair, wide)

        each_block(work)

    def add_point(mixed, total):
        flat = mixed[0:height].reshape(-1, channels).astype(BF16)
        total[...] += lax.dot_general(
            flat, grad_flat[...], (((0,), (0,)), ((), ())), preferred_element_type=F32
        )

    def share(part, step):
        source = (give_three, give_five, give_taps)[part]
        target = (take_three, take_five, take_taps)[part]
        peer = lax.rem(img + step, group)
        return pltpu.make_async_remote_copy(
            src_ref=source.at[peer],
            dst_ref=target.at[step],
            send_sem=give_sem.at[part, step],
            recv_sem=take_sem.at[part, step],
            device_id={"sec": sec, "img": peer},
            device_id_type=MESH,
        )

    prepare(0)
    forward()
    callers = group + 1 - bottom.astype(jnp.int32) - top.astype(jnp.int32)
    pl.semaphore_wait(barrier, callers)

    first_copy(0).wait()
    first_copy(1).wait()

    def turn_work(turn, carry):
        spread_grad(turn)
        pull(point_five, even_five, odd_five)

        @pl.when(turn > 0)
        def _():
            arrive(turn, 1)

        through_five(turn, outbox.at[turn, 0])

        @pl.when(not_bottom)
        def _():
            hop(turn, 0).start()

        pull(point_three, even_three, odd_three)
        through_three(outbox.at[turn, 1])

        @pl.when(not_bottom)
        def _():
            hop(turn, 1).start()

        add_point(mixed_five, total_five)
        add_point(mixed_three, total_three)
        add_taps()
        prepare(turn + 1)
        forward()
        arrive(turn + 1, 0)
        return carry

    lax.fori_loop(0, turns - 1, turn_work, 0)

    end = turns - 1
    spread_grad(end)
    for part, mixed, total, give in (
        (0, mixed_three, total_three, give_three),
        (1, mixed_five, total_five, give_five),
    ):
        add_point(mixed, total)
        for peer in range(group):
            give[peer] = (total[peer * rows : (peer + 1) * rows] * factor).astype(BF16)
        for step in range(1, group):
            share(part, step).start()
    pull(point_five, even_five, odd_five)
    pull(point_three, even_three, odd_three)
    add_taps()
    count_five, count_three = five * five, three * three
    for sums, start, count in ((sums_five, 0, count_five), (sums_three, count_five, count_three)):
        folded = jnp.sum(sums[...], axis=1)
        sums_all[start : start + count] = folded[:, 0:channels] + folded[:, channels:]
    flipped = sums_all[...].T * factor
    for peer in range(group):
        give_taps[peer] = flipped[peer * rows : (peer + 1) * rows].astype(BF16)
    for step in range(1, group):
        share(2, step).start()
    arrive(end, 1)
    through_five(end, outgoing.at[0])
    through_three(outgoing.at[1])

    def gathered(part, give, take):
        value = give[img].astype(F32)
        for step in range(1, group):
            share(part, step).wait_recv()
            value = value + take[step].astype(F32)
        return value

    out_three[...] = gathered(0, give_three, take_three)
    out_five[...] = gathered(1, give_five, take_five)
    by_tap = gathered(2, give_taps, take_taps).T
    for tap in range(count_five):
        out_taps_five[tap] = by_tap[tap : tap + 1]
    for tap in range(count_three):
        out_taps_three[tap] = by_tap[count_five + tap : count_five + tap + 1]
    for part in range(3):
        for step in range(1, group):
            share(part, step).wait_send()

    @pl.when(not_bottom)
    def _():
        for turn in range(turns - 1):
            for which in range(2):
                hop(turn, which).wait_send()


def local(
    sections,
    group,
    saved_last,
    saved_older,
    arriving,
    head_adjoint,
    plan,
    depth_five,
    depth_three,
    point_five,
    point_three,
):
    turns, _, height, width, channels = saved_last.shape[1:]
    count_five, count_three = depth_five.shape[1], depth_three.shape[1]
    five, three = round(count_five**0.5), round(count_three**0.5)
    breadth = up(width + five // 2, 8)
    pairs = up(height, 2) // 2
    even = pltpu.VMEM((pairs + 2, breadth, 2 * channels), BF16)
    odd = pltpu.VMEM((pairs + 1, breadth, 2 * channels), BF16)
    rows = channels // group
    vmem = pl.BlockSpec(memory_space=pltpu.VMEM)
    smem = pl.BlockSpec(memory_space=pltpu.SMEM)
    outside = pl.BlockSpec(memory_space=pl.ANY)
    body = functools.partial(kernel_body, sections, group, (five, three))
    outgoing, grad_five, grad_three, taps_five, taps_three = pl.pallas_call(
        body,
        out_shape=(
            jax.ShapeDtypeStruct((2, 2 * pairs, width, channels), BF16),
            jax.ShapeDtypeStruct((rows, channels), F32),
            jax.ShapeDtypeStruct((rows, channels), F32),
            jax.ShapeDtypeStruct((count_five, 1, rows), F32),
            jax.ShapeDtypeStruct((count_three, 1, rows), F32),
        ),
        in_specs=[smem, vmem, vmem, *[outside] * 4, *[vmem] * 4],
        out_specs=(vmem,) * 5,
        scratch_shapes=[
            pltpu.VMEM((turns, 2, 2 * pairs, width, channels), BF16),
            pltpu.VMEM((turns - 1, 2, 2 * pairs, width, channels), BF16),
            pltpu.VMEM((2 * pairs + 2, breadth, channels), F32),
            *([even, odd] * 4),
            pltpu.VMEM((2 * pairs, breadth, channels), F32),
            pltpu.VMEM((height * breadth, channels), BF16),
            pltpu.VMEM((2 * pairs, breadth, channels), F32),
            pltpu.VMEM((2 * pairs, breadth, channels), F32),
            pltpu.VMEM((count_five, 8, 2 * channels), BF16),
            pltpu.VMEM((count_three, 8, 2 * channels), BF16),
            pltpu.VMEM((channels, channels), F32),
            pltpu.VMEM((channels, channels), F32),
            pltpu.VMEM((count_five, 8, 2 * channels), F32),
            pltpu.VMEM((count_three, 8, 2 * channels), F32),
            pltpu.VMEM((LANES, channels), F32),
            pltpu.VMEM((group, rows, channels), BF16),
            pltpu.VMEM((group, rows, channels), BF16),
            pltpu.VMEM((group, rows, LANES), BF16),
            pltpu.VMEM((group, rows, channels), BF16),
            pltpu.VMEM((group, rows, channels), BF16),
            pltpu.VMEM((group, rows, LANES), BF16),
            pltpu.SemaphoreType.DMA((turns, 2)),
            pltpu.SemaphoreType.DMA((turns - 1, 2)),
            pltpu.SemaphoreType.DMA((turns - 1, 2)),
            pltpu.SemaphoreType.DMA((3, group)),
            pltpu.SemaphoreType.DMA((3, group)),
        ],
        compiler_params=pltpu.CompilerParams(collective_id=0, has_side_effects=True),
    )(
        plan,
        saved_last.reshape(turns, height, width, channels),
        saved_older.reshape(turns, height, width, channels),
        arriving[0, 0, 0],
        arriving[0, 1, 0],
        head_adjoint[:, 0, 0],
        head_adjoint[:, 1, 0],
        depth_five[0],
        depth_three[0],
        point_five[0],
        point_three[0],
    )
    return (
        outgoing[:, :height].reshape(1, 2, 1, height, width, channels),
        grad_five[None],
        taps_five.transpose(1, 2, 0),
        grad_three[None],
        taps_three.transpose(1, 2, 0),
    )


def solution(mesh):
    placed = (
        P("sec", None, "img", None, None, None),
        P("sec", None, "img", None, None, None),
        P("sec", None, "img", None, None, None),
        P(None, None, "img", None, None, None),
        P("sec", None),
        P("sec", None, None),
        P("sec", None, None),
        P("sec", None, None),
        P("sec", None, None),
    )
    return jax.shard_map(
        functools.partial(local, mesh.shape["sec"], mesh.shape["img"]),
        mesh=mesh,
        in_specs=placed,
        out_specs=(
            P("sec", None, "img", None, None, None),
            P("sec", "img", None),
            P("sec", "img", None),
            P("sec", "img", None),
            P("sec", "img", None),
        ),
        check_vma=False,
    )
```
